32 devices in a mesh: row: 8 (over z, x), ch: 4 (over y, core).
Axes of the slice: x: 2, y: 2, z: 4, core: 2. Of those that a mesh axis runs over, the one named last changes fastest.
Arguments:
- pair_rep: bfloat16 [128, 8, 8], P('ch', 'row'), may hold values from -6 to 6
- residue_mask: int32 [8], replicated, may hold values 0 or 1
- chain_ids: int32 [8], replicated, may hold values from 0 to 3, never falling along the last dimension, each value on 1 to 4 neighbouring positions
- in_gain: float32 [2, 128], replicated, may hold values from 0.5 to 1.5
- in_bias: float32 [2, 128], replicated, may hold values from -3 to 3
- w_proj: bfloat16 [2, 128, 4, 128], P(None, None, None, 'ch'), may hold values from -0.5 to 0.5
- w_gate: bfloat16 [2, 128, 128], P(None, None, 'ch'), may hold values from -0.5 to 0.5
- pair_bias: float32 [2, 128], P(None, 'ch'), may hold values from -4 to 4
- out_gain: float32 [2, 128], P(None, 'ch'), may hold values from 0.5 to 1.5
- out_bias: float32 [2, 128], P(None, 'ch'), may hold values from -3 to 3
- w_out: bfloat16 [2, 128, 128], P(None, 'ch'), may hold values from -0.5 to 0.5
Outputs:
- pair_out: bfloat16 [128, 8, 8], P('ch', 'row')
The draws below stay inside these ranges and needn't reach their ends.
Inputs may be any that keep to these rules, and one draw needn't show every extreme that they name: `chain_ids`: chain numbers never fall along the residues; each chain has 1 to 4 residues.
All inputs are finite; a program needn't handle non-finite values.
Results may differ from the reference program's by a relative error of at most 0.013.
Values may be sent and summed in bfloat16 or wider, within the bound.
A program may use at most 64 MiB of HBM per device.

```python
import math
import jax
import jax.numpy as jnp
import numpy as np
from jax import lax

C = 128
CH = 128
N = 8


def place_ends(array, own_key, least, largest):
    longest = array.shape.index(max(array.shape))
    spots = []
    for shift in (0, 1):
        where = [jax.random.randint(jax.random.fold_in(own_key, axis), (), 0, length) for axis, length in enumerate(array.shape)]
        where[longest] = (where[longest] + shift) % array.shape[longest]
        spots.append(tuple(where))
    return array.at[spots[0]].set(least).at[spots[1]].set(largest)


def shard_levels(key, shape, cuts, smallest, largest):
    level = 1.0
    for position, shards_of in cuts:
        draws = jax.random.uniform(jax.random.fold_in(jax.random.fold_in(key, 6), position), (shards_of,), jnp.float32, smallest / len(cuts), largest / len(cuts))
        level = level * jnp.repeat(jnp.exp(draws), shape[position] // shards_of).reshape((-1,) + (1,) * (len(shape) - 1 - position))
    return level


def split_up(amount, total, reach, lean):
    weights = [(1 << 20) // math.isqrt(grade ** lean) + 1 for grade in range(2, amount + 1)]
    spare, counts = total - reach - (amount - 1), [1] * (amount - 1)
    while spare > 0:
        movable = [i for i in range(amount - 1) if counts[i] < reach]
        whole, left = sum([weights[i] for i in movable]), spare
        for i in movable:
            addition = min(reach - counts[i], max(1, left * weights[i] // whole), spare)
            counts[i] = counts[i] + addition
            spare = spare - addition
    return np.array([reach] + counts)


def uneven(rng, amount, total, bound, skew):
    if amount == 2:
        one = jax.random.randint(rng, (), max(1, total - bound), min(bound, total - 1) + 1)
        return jnp.stack([one, total - one])
    lengths = jnp.asarray(split_up(amount, total, bound, skew), jnp.int32)
    twos = (amount - 1) // 2
    source_of, receiver = lengths[1:1 + 2 * twos:2], lengths[2:2 + 2 * twos:2]
    slack = jnp.minimum(source_of - 1, bound - receiver)
    passed = jax.random.randint(jax.random.fold_in(rng, 1), (twos,), 0, 1 << 20) % (slack + 1)
    lengths = lengths.at[1:1 + 2 * twos:2].set(source_of - passed).at[2:2 + 2 * twos:2].set(receiver + passed)
    return lengths[jax.random.permutation(jax.random.fold_in(rng, 2), amount)]


def bell_draw(own_key, shape, scale, bound, split=(), held_as=jnp.bfloat16):
    drawn = scale * jax.random.normal(own_key, shape, jnp.float32)
    if split:
        drawn = drawn * shard_levels(own_key, shape, split, -0.22, 0.18)
    return jnp.clip(drawn, -bound, bound).astype(held_as)


def setup_inputs(seed: int = 0) -> dict:
    arg_keys = jax.random.split(jax.random.key(seed), 12)
    return {
        "pair_rep": bell_draw(arg_keys[0], (C, N, N), 1.0, 6.0, ((0, 4), (1, 8))),
        "residue_mask": place_ends((jax.random.randint(arg_keys[1], (N,), 0, 8) < 7).astype(jnp.int32), jax.random.fold_in(arg_keys[1], 1), 0, 1),
        "chain_ids": jnp.searchsorted(jnp.cumsum(uneven(arg_keys[2], 4, N, N // 2, 1)), jnp.arange(N), side="right").astype(jnp.int32),
        "in_gain": jnp.clip(1.0 + 0.1 * jax.random.normal(arg_keys[3], (2, C), jnp.float32), 0.5, 1.5),
        "in_bias": bell_draw(arg_keys[4], (2, C), 0.5, 3.0, (), jnp.float32),
        "w_proj": bell_draw(arg_keys[5], (2, C, 4, CH), C ** -0.5, 0.5, ((3, 4),)),
        "w_gate": bell_draw(arg_keys[6], (2, C, C), C ** -0.5, 0.5, ((2, 4),)),
        "pair_bias": bell_draw(arg_keys[7], (2, C), 1.0, 4.0, ((1, 4),), jnp.float32),
        "out_gain": jnp.clip(1.0 + 0.1 * jax.random.normal(arg_keys[8], (2, CH), jnp.float32), 0.5, 1.5),
        "out_bias": bell_draw(arg_keys[9], (2, CH), 0.5, 3.0, ((1, 4),), jnp.float32),
        "w_out": bell_draw(arg_keys[10], (2, CH, C), CH ** -0.5, 0.5, ((1, 4),)),
    }


epsilon = 1e-05

def channel_norm(values, norm_gain, norm_bias):
    mean_val = lax.optimization_barrier(jnp.mean(values, axis=0))
    variance = lax.optimization_barrier(jnp.mean(values * values, axis=0)) - mean_val * mean_val
    return (values - mean_val) * lax.rsqrt(variance + epsilon) * norm_gain[:, None, None] + norm_bias[:, None, None]

def reference(pair_rep, residue_mask, chain_ids, in_gain, in_bias, w_proj, w_gate, pair_bias, out_gain, out_bias, w_out):
    mask_float = residue_mask.astype(jnp.float32)
    pair_mask = mask_float[:, None] * mask_float[None, :]
    same_chain = (chain_ids[:, None] == chain_ids[None, :]).astype(jnp.float32)

    def update(pair_in, layer, incoming):
        normed = channel_norm(pair_in.astype(jnp.float32), in_gain[layer], in_bias[layer]).astype(jnp.bfloat16)
        normed_f = normed.astype(jnp.float32)
        projected = jnp.einsum('cij,cpd->pdij', normed_f, w_proj[layer].astype(jnp.float32))
        left_arm = (jax.nn.sigmoid(projected[0]) * projected[1] * pair_mask).astype(jnp.bfloat16).astype(jnp.float32)
        right_arm = (jax.nn.sigmoid(projected[2]) * projected[3] * pair_mask).astype(jnp.bfloat16).astype(jnp.float32)
        if incoming:
            product_sum = jnp.einsum('dki,dkj->dij', left_arm, right_arm)
        else:
            product_sum = jnp.einsum('dik,djk->dij', left_arm, right_arm)
        normed_x = channel_norm(product_sum, out_gain[layer], out_bias[layer]).astype(jnp.bfloat16)
        mixed = jnp.einsum('dij,dc->cij', normed_x.astype(jnp.float32), w_out[layer].astype(jnp.float32))
        logits = jnp.einsum('cij,cd->dij', normed_f, w_gate[layer].astype(jnp.float32)) + pair_bias[layer][:, None, None] * same_chain[None]
        return (pair_in.astype(jnp.float32) + jax.nn.sigmoid(logits) * mixed).astype(jnp.bfloat16)
    middle = update(pair_rep, 0, False)
    return update(middle, 1, True)
```

```python
import functools
import jax
import jax.numpy as jnp
from jax import lax
from jax.experimental import pallas as pl
from jax.experimental.pallas import tpu as pltpu
from jax.sharding import PartitionSpec as P

epsilon = 1e-05
MESH = pl.DeviceIdType.MESH
F32 = jnp.float32
BF16 = jnp.bfloat16


def lane_norm(values, gain, bias):
    mean_val = jnp.mean(values, axis=-1, keepdims=True)
    variance = jnp.mean(values * values, axis=-1, keepdims=True) - mean_val * mean_val
    return ((values - mean_val) * lax.rsqrt(variance + epsilon) * gain + bias).astype(BF16)


def dot_nt(a, b):
    return lax.dot_general(a, b, (((1,), (1,)), ((), ())), preferred_element_type=F32)


def dot_nn(a, b):
    return lax.dot_general(a, b, (((1,), (0,)), ((), ())), preferred_element_type=F32)


def window_kernel(
    rows,
    chs,
    mask_ref,
    chain_ref,
    small_ref,
    in_gain_ref,
    in_bias_ref,
    weights_ref,
    out_ref,
    small_buf,
    weights_buf,
    pair_buf,
    left_buf,
    right_buf,
    middle_buf,
    normed_buf,
    small_send,
    small_recv,
    weights_send,
    weights_recv,
    row_send,
    row_recv,
    own_sem,
):
    n = pair_buf.shape[0]
    lanes = pair_buf.shape[2]
    block = lanes // chs
    row = lax.axis_index("row")
    ch = lax.axis_index("ch")

    own_copies = [pltpu.make_async_copy(small_ref, small_buf.at[ch], own_sem.at[0])]
    for u in range(2):
        own_copies.append(
            pltpu.make_async_copy(weights_ref.at[u], weights_buf.at[u, ch], own_sem.at[1 + u])
        )
    for copy in own_copies:
        copy.start()

    barrier = pltpu.get_barrier_semaphore()
    for step in range(1, chs):
        pl.semaphore_signal(
            barrier, inc=1, device_id=(row, lax.rem(ch + step, chs)), device_id_type=MESH
        )
    for step in range(1, rows):
        pl.semaphore_signal(
            barrier, inc=1, device_id=(lax.rem(row + step, rows), ch), device_id_type=MESH
        )
    pl.semaphore_wait(barrier, chs - 1 + rows - 1)

    small_copies = []
    for step in range(1, chs):
        copy = pltpu.make_async_remote_copy(
            src_ref=small_ref,
            dst_ref=small_buf.at[ch],
            send_sem=small_send.at[step - 1],
            recv_sem=small_recv.at[step - 1],
            device_id=(row, lax.rem(ch + step, chs)),
            device_id_type=MESH,
        )
        copy.start()
        small_copies.append(copy)
    weight_copies = []
    for u in range(2):
        group = []
        for step in range(1, chs):
            copy = pltpu.make_async_remote_copy(
                src_ref=weights_ref.at[u],
                dst_ref=weights_buf.at[u, ch],
                send_sem=weights_send.at[u, step - 1],
                recv_sem=weights_recv.at[u, step - 1],
                device_id=(row, lax.rem(ch + step, chs)),
                device_id_type=MESH,
            )
            copy.start()
            group.append(copy)
        weight_copies.append(group)

    own_copies[0].wait()
    for copy in small_copies:
        copy.wait_recv()
    pair_buf[row] = jnp.concatenate([small_buf[m, :n, :] for m in range(chs)], axis=1)

    row_copies = []
    for step in range(1, rows):
        copy = pltpu.make_async_remote_copy(
            src_ref=pair_buf.at[row],
            dst_ref=pair_buf.at[row],
            send_sem=row_send.at[step - 1],
            recv_sem=row_recv.at[step - 1],
            device_id=(lax.rem(row + step, rows), ch),
            device_id_type=MESH,
        )
        copy.start()
        row_copies.append(copy)

    vectors = jnp.concatenate([small_buf[m, n:, :] for m in range(chs)], axis=1)
    place = lax.broadcasted_iota(jnp.int32, (n, lanes), 0)
    mask_j = jnp.zeros((n, lanes), jnp.int32)
    chain_j = jnp.zeros((n, lanes), jnp.int32)
    for j in range(n):
        mask_j = jnp.where(place == j, mask_ref[j], mask_j)
        chain_j = jnp.where(place == j, chain_ref[j], chain_j)
    pair_mask = jnp.concatenate([(mask_j * mask_ref[i]).astype(F32) for i in range(n)], axis=0)
    same_chain = jnp.concatenate(
        [jnp.where(chain_j == chain_ref[i], 1.0, 0.0).astype(F32) for i in range(n)], axis=0
    )
    same_here = jnp.where(chain_j == chain_ref[row], 1.0, 0.0).astype(F32)

    def weight(u, part):
        return weights_buf[u, :, part * block : (part + 1) * block, :].reshape(lanes, lanes)

    def arms(u, normed):
        left = jax.nn.sigmoid(dot_nt(normed, weight(u, 0))) * dot_nt(normed, weight(u, 1))
        right = jax.nn.sigmoid(dot_nt(normed, weight(u, 2))) * dot_nt(normed, weight(u, 3))
        left_buf[...] = (left * pair_mask).astype(BF16).astype(F32)
        right_buf[...] = (right * pair_mask).astype(BF16).astype(F32)

    def update(u, pair, normed, product, same):
        xn = lane_norm(product, vectors[2 + u : 3 + u, :], vectors[4 + u : 5 + u, :])
        mixed = dot_nn(xn, weight(u, 5))
        gate = jax.nn.sigmoid(dot_nt(normed, weight(u, 4)) + vectors[u : u + 1, :] * same)
        return (pair + gate * mixed).astype(BF16)

    for copy in row_copies:
        copy.wait_recv()
    pair = pair_buf[...].reshape(n * n, lanes)
    normed = lane_norm(pair, in_gain_ref[0:1, :], in_bias_ref[0:1, :])
    own_copies[1].wait()
    for copy in weight_copies[0]:
        copy.wait_recv()
    arms(0, normed)
    right_k = [right_buf[pl.ds(k, n, stride=n), :] for k in range(n)]
    product = []
    for i in range(n):
        total = left_buf[i * n : i * n + 1, :] * right_k[0]
        for k in range(1, n):
            total = total + left_buf[i * n + k : i * n + k + 1, :] * right_k[k]
        product.append(total)
    middle = update(0, pair, normed, jnp.concatenate(product, axis=0), same_chain).astype(F32)
    middle_buf[...] = middle

    normed = lane_norm(middle, in_gain_ref[1:2, :], in_bias_ref[1:2, :])
    normed_buf[...] = normed.astype(F32)
    own_copies[2].wait()
    for copy in weight_copies[1]:
        copy.wait_recv()
    arms(1, normed)
    total = left_buf[pl.ds(row, 1), :] * right_buf[0:n, :]
    for k in range(1, n):
        total = total + left_buf[pl.ds(k * n + row, 1), :] * right_buf[k * n : (k + 1) * n, :]
    here = pl.ds(pl.multiple_of(row * n, n), n)
    result = update(1, middle_buf[here, :], normed_buf[here, :].astype(BF16), total, same_here)

    picked = lax.broadcasted_iota(jnp.int32, (block, lanes), 1)
    wanted = lax.broadcasted_iota(jnp.int32, (block, lanes), 0) + ch * block
    chosen = jnp.where(picked == wanted, 1.0, 0.0).astype(BF16)
    out_ref[...] = dot_nt(chosen, result).astype(BF16)

    for copy in small_copies + weight_copies[0] + weight_copies[1] + row_copies:
        copy.wait_send()


def window_body(
    rows,
    chs,
    pair_rep,
    residue_mask,
    chain_ids,
    in_gain,
    in_bias,
    w_proj,
    w_gate,
    pair_bias,
    out_gain,
    out_bias,
    w_out,
):
    block, _, n = pair_rep.shape
    lanes = in_gain.shape[1]
    layers, _, parts, _ = w_proj.shape
    weights = jnp.concatenate(
        [
            jnp.transpose(w_proj, (0, 2, 3, 1)).reshape(layers, parts * block, lanes),
            jnp.swapaxes(w_gate, 1, 2),
            w_out,
        ],
        axis=1,
    )
    small = jnp.concatenate(
        [
            jnp.swapaxes(pair_rep[:, 0, :], 0, 1).astype(F32),
            pair_bias,
            out_gain,
            out_bias,
            jnp.zeros((2, block), F32),
        ],
        axis=0,
    )
    vmem = pl.BlockSpec(memory_space=pltpu.VMEM)
    smem = pl.BlockSpec(memory_space=pltpu.SMEM)
    dma = pltpu.SemaphoreType.DMA
    out = pl.pallas_call(
        functools.partial(window_kernel, rows, chs),
        out_shape=jax.ShapeDtypeStruct((block, n), BF16),
        in_specs=[smem, smem, vmem, vmem, vmem, vmem],
        out_specs=vmem,
        scratch_shapes=[
            pltpu.VMEM((chs,) + small.shape, F32),
            pltpu.VMEM((layers, chs) + weights.shape[1:], BF16),
            pltpu.VMEM((n, n, lanes), F32),
            pltpu.VMEM((n * n, lanes), F32),
            pltpu.VMEM((n * n, lanes), F32),
            pltpu.VMEM((n * n, lanes), F32),
            pltpu.VMEM((n * n, lanes), F32),
            dma((chs - 1,)),
            dma((chs - 1,)),
            dma((layers, chs - 1)),
            dma((layers, chs - 1)),
            dma((rows - 1,)),
            dma((rows - 1,)),
            dma((1 + layers,)),
        ],
        compiler_params=pltpu.CompilerParams(collective_id=0, has_side_effects=True),
    )(residue_mask, chain_ids, small, in_gain, in_bias, weights)
    return out[:, None, :]


def channel_norm(values, norm_gain, norm_bias):
    mean_val = jnp.mean(values, axis=0)
    variance = jnp.mean(values * values, axis=0) - mean_val * mean_val
    return (values - mean_val) * lax.rsqrt(variance + epsilon) * norm_gain[
        :, None, None
    ] + norm_bias[:, None, None]


def prepare(
    pair_local, layer, in_gain, in_bias, w_proj, w_gate, pair_bias, mask_rows, mask_cols, same_chain
):
    full_pair = lax.all_gather(pair_local, "ch", axis=0, tiled=True)
    normed = channel_norm(full_pair.astype(jnp.float32), in_gain[layer], in_bias[layer]).astype(
        jnp.bfloat16
    )
    projected = jnp.einsum(
        "cij,cpd->pdij", normed, w_proj[layer], preferred_element_type=jnp.float32
    )
    pair_mask = mask_rows[:, None] * mask_cols[None, :]
    first_arm = (jax.nn.sigmoid(projected[0]) * projected[1] * pair_mask).astype(jnp.bfloat16)
    second_arm = (jax.nn.sigmoid(projected[2]) * projected[3] * pair_mask).astype(jnp.bfloat16)
    logits = jnp.einsum("cij,cd->dij", normed, w_gate[layer], preferred_element_type=jnp.float32)
    logits = logits + pair_bias[layer][:, None, None] * same_chain[None]
    return (first_arm, second_arm, jax.nn.sigmoid(logits))


def finish(product_sum, gating, layer, out_gain, out_bias, w_out):
    totals = lax.psum(
        (jnp.sum(product_sum, axis=0), jnp.sum(product_sum * product_sum, axis=0)), "ch"
    )
    channels = product_sum.shape[0] * lax.axis_size("ch")
    mean_val = totals[0] / channels
    variance = totals[1] / channels - mean_val * mean_val
    scaled = (product_sum - mean_val) * lax.rsqrt(variance + epsilon)
    normed = (scaled * out_gain[layer][:, None, None] + out_bias[layer][:, None, None]).astype(
        jnp.bfloat16
    )
    columns = w_out[layer]
    mixed = lax.psum_scatter(
        jnp.einsum("dij,dc->cij", normed, columns, preferred_element_type=jnp.float32).astype(
            jnp.bfloat16
        ),
        "ch",
        scatter_dimension=0,
        tiled=True,
    ).astype(jnp.float32)
    return gating * mixed


def body(
    pair_rep,
    residue_mask,
    chain_ids,
    in_gain,
    in_bias,
    w_proj,
    w_gate,
    pair_bias,
    out_gain,
    out_bias,
    w_out,
):
    rows_here = pair_rep.shape[1]
    row_start = lax.axis_index("row") * rows_here
    mask_cols = residue_mask.astype(jnp.float32)
    mask_rows = lax.dynamic_slice_in_dim(mask_cols, row_start, rows_here)
    chain_rows = lax.dynamic_slice_in_dim(chain_ids, row_start, rows_here)
    same_chain = (chain_rows[:, None] == chain_ids[None, :]).astype(jnp.float32)
    first_arm, second_arm, gating = prepare(
        pair_rep, 0, in_gain, in_bias, w_proj, w_gate, pair_bias, mask_rows, mask_cols, same_chain
    )
    product_sum = jnp.einsum(
        "cik,cjk->cij",
        first_arm,
        lax.all_gather(second_arm, "row", axis=1, tiled=True),
        preferred_element_type=jnp.float32,
    )
    middle = (
        pair_rep.astype(jnp.float32) + finish(product_sum, gating, 0, out_gain, out_bias, w_out)
    ).astype(jnp.bfloat16)
    in_first, in_second, in_gating = prepare(
        middle, 1, in_gain, in_bias, w_proj, w_gate, pair_bias, mask_rows, mask_cols, same_chain
    )
    exchanged_left = lax.all_to_all(in_first, "row", split_axis=2, concat_axis=1, tiled=True)
    left_rows = jnp.swapaxes(exchanged_left, 1, 2)
    in_product = jnp.einsum(
        "cik,ckj->cij",
        left_rows,
        lax.all_gather(in_second, "row", axis=1, tiled=True),
        preferred_element_type=jnp.float32,
    )
    update = finish(in_product, in_gating, 1, out_gain, out_bias, w_out)
    return (middle.astype(jnp.float32) + update).astype(jnp.bfloat16)


def choose(rows, chs, *args):
    pair_rep, in_gain = args[0], args[3]
    n, lanes = pair_rep.shape[2], in_gain.shape[1]
    one_tile = pair_rep.shape[1] == 1 and n == rows == 8 and lanes == 128
    if one_tile and chs > 1 and args[5].shape[1] == pair_rep.shape[0] * chs:
        return window_body(rows, chs, *args)
    return body(*args)


def solution(mesh):
    return jax.shard_map(
        functools.partial(choose, mesh.shape["row"], mesh.shape["ch"]),
        mesh=mesh,
        in_specs=(
            P("ch", "row", None),
            P(),
            P(),
            P(),
            P(),
            P(None, None, None, "ch"),
            P(None, None, "ch"),
            P(None, "ch"),
            P(None, "ch"),
            P(None, "ch"),
            P(None, "ch", None),
        ),
        out_specs=P("ch", "row", None),
        check_vma=False,
    )
```

```python
import functools
import jax
import jax.numpy as jnp
from jax import lax
from jax.experimental import pallas as pl
from jax.experimental.pallas import tpu as pltpu
from jax.sharding import PartitionSpec as P

epsilon = 1e-05
MESH = pl.DeviceIdType.MESH
F32 = jnp.float32
BF16 = jnp.bfloat16


def lane_norm(values, gain, bias):
    mean_val = jnp.mean(values, axis=-1, keepdims=True)
    variance = jnp.mean(values * values, axis=-1, keepdims=True) - mean_val * mean_val
    return ((values - mean_val) * lax.rsqrt(variance + epsilon) * gain + bias).astype(BF16)


def dot_nt(a, b):
    return lax.dot_general(a, b, (((1,), (1,)), ((), ())), preferred_element_type=F32)


def dot_nn(a, b):
    return lax.dot_general(a, b, (((1,), (0,)), ((), ())), preferred_element_type=F32)


def window_kernel(
    rows,
    chs,
    mask_ref,
    chain_ref,
    pair_ref,
    in_gain_ref,
    in_bias_ref,
    proj_ref,
    gate_ref,
    bias_ref,
    gain_ref,
    offset_ref,
    mix_ref,
    out_ref,
    block_buf,
    proj_buf,
    gate_buf,
    mix_buf,
    vector_buf,
    pair_buf,
    left_buf,
    right_buf,
    middle_buf,
    normed_buf,
    block_send,
    block_recv,
    vector_send,
    vector_recv,
    weight_send,
    weight_recv,
    row_send,
    row_recv,
    own_sem,
):
    n = pair_buf.shape[0]
    lanes = pair_buf.shape[2]
    block = lanes // chs
    row = lax.axis_index("row")
    ch = lax.axis_index("ch")

    barrier = pltpu.get_barrier_semaphore()
    for step in range(1, chs):
        pl.semaphore_signal(
            barrier, inc=1, device_id=(row, lax.rem(ch + step, chs)), device_id_type=MESH
        )
    for step in range(1, rows):
        pl.semaphore_signal(
            barrier, inc=1, device_id=(lax.rem(row + step, rows), ch), device_id_type=MESH
        )

    first = [(pair_ref, block_buf.at[ch], 0, block_send, block_recv)]
    vectors_out = [
        (ref, vector_buf.at[t, ch], 1 + t, vector_send.at[t], vector_recv.at[t])
        for t, ref in enumerate((bias_ref, gain_ref, offset_ref))
    ]
    weights_out = []
    for u in range(2):
        group = []
        for t, (ref, buf) in enumerate(
            ((proj_ref, proj_buf), (gate_ref, gate_buf), (mix_ref, mix_buf))
        ):
            group.append(
                (
                    ref.at[u],
                    buf.at[u, ch],
                    4 + 3 * u + t,
                    weight_send.at[u, t],
                    weight_recv.at[u, t],
                )
            )
        weights_out.append(group)

    def keep(items):
        copies = [pltpu.make_async_copy(src, dst, own_sem.at[k]) for src, dst, k, _, _ in items]
        for copy in copies:
            copy.start()
        return copies

    def spread(items):
        copies = []
        for src, dst, _, send, recv in items:
            for step in range(1, chs):
                copy = pltpu.make_async_remote_copy(
                    src_ref=src,
                    dst_ref=dst,
                    send_sem=send.at[step - 1],
                    recv_sem=recv.at[step - 1],
                    device_id=(row, lax.rem(ch + step, chs)),
                    device_id_type=MESH,
                )
                copy.start()
                copies.append(copy)
        return copies

    def arrive(own, remote):
        for copy in own:
            copy.wait()
        for copy in remote:
            copy.wait_recv()

    own_first = keep(first)
    own_weights = [keep(weights_out[0] + vectors_out), keep(weights_out[1])]

    place = lax.broadcasted_iota(jnp.int32, (n, lanes), 0)
    mask_j = jnp.zeros((n, lanes), jnp.int32)
    chain_j = jnp.zeros((n, lanes), jnp.int32)
    for j in range(n):
        mask_j = jnp.where(place == j, mask_ref[j], mask_j)
        chain_j = jnp.where(place == j, chain_ref[j], chain_j)
    pair_mask = jnp.concatenate([(mask_j * mask_ref[i]).astype(F32) for i in range(n)], axis=0)
    same_chain = jnp.concatenate(
        [jnp.where(chain_j == chain_ref[i], 1.0, 0.0).astype(F32) for i in range(n)], axis=0
    )
    same_here = jnp.where(chain_j == chain_ref[row], 1.0, 0.0).astype(F32)

    pl.semaphore_wait(barrier, chs - 1 + rows - 1)
    remote_first = spread(first)
    remote_weights = [spread(weights_out[0] + vectors_out), spread(weights_out[1])]

    arrive(own_first, remote_first)
    pair_buf[row] = jnp.concatenate([block_buf[m].astype(F32) for m in range(chs)], axis=1)
    row_copies = []
    for step in range(1, rows):
        copy = pltpu.make_async_remote_copy(
            src_ref=pair_buf.at[row],
            dst_ref=pair_buf.at[row],
            send_sem=row_send.at[step - 1],
            recv_sem=row_recv.at[step - 1],
            device_id=(lax.rem(row + step, rows), ch),
            device_id_type=MESH,
        )
        copy.start()
        row_copies.append(copy)

    def projection(u, part):
        here = slice(part * block, (part + 1) * block)
        return proj_buf[u, :, here, :].reshape(lanes, lanes)

    def vector(t, u):
        return jnp.concatenate([vector_buf[t, m, u : u + 1, :] for m in range(chs)], axis=1)

    def arms(u, normed):
        left = jax.nn.sigmoid(dot_nt(normed, projection(u, 0))) * dot_nt(normed, projection(u, 1))
        right = jax.nn.sigmoid(dot_nt(normed, projection(u, 2))) * dot_nt(normed, projection(u, 3))
        left_buf[...] = (left * pair_mask).astype(BF16).astype(F32)
        right_buf[...] = (right * pair_mask).astype(BF16).astype(F32)

    def update(u, pair, normed, product, same):
        xn = lane_norm(product, vector(1, u), vector(2, u))
        mixed = dot_nn(xn, mix_buf[u].reshape(lanes, lanes))
        logits = dot_nt(normed, gate_buf[u].reshape(lanes, lanes)) + vector(0, u) * same
        return (pair + jax.nn.sigmoid(logits) * mixed).astype(BF16)

    arrive([], row_copies)
    pair = pair_buf[...].reshape(n * n, lanes)
    normed = lane_norm(pair, in_gain_ref[0:1, :], in_bias_ref[0:1, :])
    arrive(own_weights[0], remote_weights[0])
    arms(0, normed)
    right_k = [right_buf[pl.ds(k, n, stride=n), :] for k in range(n)]
    product = []
    for i in range(n):
        total = left_buf[i * n : i * n + 1, :] * right_k[0]
        for k in range(1, n):
            total = total + left_buf[i * n + k : i * n + k + 1, :] * right_k[k]
        product.append(total)
    middle = update(0, pair, normed, jnp.concatenate(product, axis=0), same_chain).astype(F32)
    middle_buf[...] = middle

    normed = lane_norm(middle, in_gain_ref[1:2, :], in_bias_ref[1:2, :])
    normed_buf[...] = normed.astype(F32)
    arrive(own_weights[1], remote_weights[1])
    arms(1, normed)
    total = left_buf[pl.ds(row, 1), :] * right_buf[0:n, :]
    for k in range(1, n):
        total = total + left_buf[pl.ds(k * n + row, 1), :] * right_buf[k * n : (k + 1) * n, :]
    here = pl.ds(pl.multiple_of(row * n, n), n)
    result = update(1, middle_buf[here, :], normed_buf[here, :].astype(BF16), total, same_here)

    picked = lax.broadcasted_iota(jnp.int32, (block, lanes), 1)
    wanted = lax.broadcasted_iota(jnp.int32, (block, lanes), 0) + ch * block
    chosen = jnp.where(picked == wanted, 1.0, 0.0).astype(BF16)
    out_ref[...] = dot_nt(result, chosen).astype(BF16)

    for copy in remote_first + remote_weights[0] + remote_weights[1] + row_copies:
        copy.wait_send()


def window_body(
    rows,
    chs,
    pair_rep,
    residue_mask,
    chain_ids,
    in_gain,
    in_bias,
    w_proj,
    w_gate,
    pair_bias,
    out_gain,
    out_bias,
    w_out,
):
    block, _, n = pair_rep.shape
    lanes = in_gain.shape[1]
    layers, _, parts, _ = w_proj.shape
    vmem = pl.BlockSpec(memory_space=pltpu.VMEM)
    smem = pl.BlockSpec(memory_space=pltpu.SMEM)
    dma = pltpu.SemaphoreType.DMA
    out = pl.pallas_call(
        functools.partial(window_kernel, rows, chs),
        out_shape=jax.ShapeDtypeStruct((n, block), BF16),
        in_specs=[smem, smem] + [vmem] * 9,
        out_specs=vmem,
        scratch_shapes=[
            pltpu.VMEM((chs, n, block), BF16),
            pltpu.VMEM((layers, chs, parts * block, lanes), BF16),
            pltpu.VMEM((layers, chs, block, lanes), BF16),
            pltpu.VMEM((layers, chs, block, lanes), BF16),
            pltpu.VMEM((3, chs, layers, block), F32),
            pltpu.VMEM((n, n, lanes), F32),
            pltpu.VMEM((n * n, lanes), F32),
            pltpu.VMEM((n * n, lanes), F32),
            pltpu.VMEM((n * n, lanes), F32),
            pltpu.VMEM((n * n, lanes), F32),
            dma((chs - 1,)),
            dma((chs - 1,)),
            dma((3, chs - 1)),
            dma((3, chs - 1)),
            dma((layers, 3, chs - 1)),
            dma((layers, 3, chs - 1)),
            dma((rows - 1,)),
            dma((rows - 1,)),
            dma((4 + 3 * layers,)),
        ],
        compiler_params=pltpu.CompilerParams(collective_id=0, has_side_effects=True),
    )(
        residue_mask,
        chain_ids,
        jnp.swapaxes(pair_rep[:, 0, :], 0, 1),
        in_gain,
        in_bias,
        jnp.transpose(w_proj, (0, 2, 3, 1)).reshape(layers, parts * block, lanes),
        jnp.swapaxes(w_gate, 1, 2),
        pair_bias,
        out_gain,
        out_bias,
        w_out,
    )
    return jnp.swapaxes(out, 0, 1)[:, None, :]


def channel_norm(values, norm_gain, norm_bias):
    mean_val = jnp.mean(values, axis=0)
    variance = jnp.mean(values * values, axis=0) - mean_val * mean_val
    return (values - mean_val) * lax.rsqrt(variance + epsilon) * norm_gain[
        :, None, None
    ] + norm_bias[:, None, None]


def prepare(
    pair_local, layer, in_gain, in_bias, w_proj, w_gate, pair_bias, mask_rows, mask_cols, same_chain
):
    full_pair = lax.all_gather(pair_local, "ch", axis=0, tiled=True)
    normed = channel_norm(full_pair.astype(jnp.float32), in_gain[layer], in_bias[layer]).astype(
        jnp.bfloat16
    )
    projected = jnp.einsum(
        "cij,cpd->pdij", normed, w_proj[layer], preferred_element_type=jnp.float32
    )
    pair_mask = mask_rows[:, None] * mask_cols[None, :]
    first_arm = (jax.nn.sigmoid(projected[0]) * projected[1] * pair_mask).astype(jnp.bfloat16)
    second_arm = (jax.nn.sigmoid(projected[2]) * projected[3] * pair_mask).astype(jnp.bfloat16)
    logits = jnp.einsum("cij,cd->dij", normed, w_gate[layer], preferred_element_type=jnp.float32)
    logits = logits + pair_bias[layer][:, None, None] * same_chain[None]
    return (first_arm, second_arm, jax.nn.sigmoid(logits))


def finish(product_sum, gating, layer, out_gain, out_bias, w_out):
    totals = lax.psum(
        (jnp.sum(product_sum, axis=0), jnp.sum(product_sum * product_sum, axis=0)), "ch"
    )
    channels = product_sum.shape[0] * lax.axis_size("ch")
    mean_val = totals[0] / channels
    variance = totals[1] / channels - mean_val * mean_val
    scaled = (product_sum - mean_val) * lax.rsqrt(variance + epsilon)
    normed = (scaled * out_gain[layer][:, None, None] + out_bias[layer][:, None, None]).astype(
        jnp.bfloat16
    )
    columns = w_out[layer]
    mixed = lax.psum_scatter(
        jnp.einsum("dij,dc->cij", normed, columns, preferred_element_type=jnp.float32).astype(
            jnp.bfloat16
        ),
        "ch",
        scatter_dimension=0,
        tiled=True,
    ).astype(jnp.float32)
    return gating * mixed


def body(
    pair_rep,
    residue_mask,
    chain_ids,
    in_gain,
    in_bias,
    w_proj,
    w_gate,
    pair_bias,
    out_gain,
    out_bias,
    w_out,
):
    rows_here = pair_rep.shape[1]
    row_start = lax.axis_index("row") * rows_here
    mask_cols = residue_mask.astype(jnp.float32)
    mask_rows = lax.dynamic_slice_in_dim(mask_cols, row_start, rows_here)
    chain_rows = lax.dynamic_slice_in_dim(chain_ids, row_start, rows_here)
    same_chain = (chain_rows[:, None] == chain_ids[None, :]).astype(jnp.float32)
    first_arm, second_arm, gating = prepare(
        pair_rep, 0, in_gain, in_bias, w_proj, w_gate, pair_bias, mask_rows, mask_cols, same_chain
    )
    product_sum = jnp.einsum(
        "cik,cjk->cij",
        first_arm,
        lax.all_gather(second_arm, "row", axis=1, tiled=True),
        preferred_element_type=jnp.float32,
    )
    middle = (
        pair_rep.astype(jnp.float32) + finish(product_sum, gating, 0, out_gain, out_bias, w_out)
    ).astype(jnp.bfloat16)
    in_first, in_second, in_gating = prepare(
        middle, 1, in_gain, in_bias, w_proj, w_gate, pair_bias, mask_rows, mask_cols, same_chain
    )
    exchanged_left = lax.all_to_all(in_first, "row", split_axis=2, concat_axis=1, tiled=True)
    left_rows = jnp.swapaxes(exchanged_left, 1, 2)
    in_product = jnp.einsum(
        "cik,ckj->cij",
        left_rows,
        lax.all_gather(in_second, "row", axis=1, tiled=True),
        preferred_element_type=jnp.float32,
    )
    update = finish(in_product, in_gating, 1, out_gain, out_bias, w_out)
    return (middle.astype(jnp.float32) + update).astype(jnp.bfloat16)


def choose(rows, chs, *args):
    pair_rep, in_gain = args[0], args[3]
    n, lanes = pair_rep.shape[2], in_gain.shape[1]
    one_tile = pair_rep.shape[1] == 1 and n == rows == 8 and lanes == 128
    if one_tile and chs > 1 and args[5].shape[1] == pair_rep.shape[0] * chs:
        return window_body(rows, chs, *args)
    return body(*args)


def solution(mesh):
    return jax.shard_map(
        functools.partial(choose, mesh.shape["row"], mesh.shape["ch"]),
        mesh=mesh,
        in_specs=(
            P("ch", "row", None),
            P(),
            P(),
            P(),
            P(),
            P(None, None, None, "ch"),
            P(None, None, "ch"),
            P(None, "ch"),
            P(None, "ch"),
            P(None, "ch"),
            P(None, "ch", None),
        ),
        out_specs=P("ch", "row", None),
        check_vma=False,
    )
```
